32 devices in a mesh: dp: 4 (over y, x), seq: 8 (over z, core).
Axes of the slice: x: 2, y: 2, z: 4, core: 2. Of those that a mesh axis runs over, the one named last changes fastest.
Arguments:
- queries: bfloat16 [4, 1024, 2048], P('dp', 'seq'), may hold values from -80 to 80
- block_memory: bfloat16 [4, 1024, 1792], P('dp', 'seq'), may hold values from -80 to 80
- neighbour_ids: int32 [4, 16, 128], P('dp', 'seq'), may hold values from 0 to 63999
- embedding: bfloat16 [896, 64000], P('seq'), may hold values from -6 to 6
- enc_query_w: bfloat16 [896, 896], P('dp'), may hold values from -0.1875 to 0.1875
- enc_out_w: bfloat16 [896, 896], P('dp'), may hold values from -0.1875 to 0.1875
- key_w: bfloat16 [896, 2048], P('dp'), may hold values from -0.1875 to 0.1875
- value_w: bfloat16 [896, 2048], P('dp'), may hold values from -0.1875 to 0.1875
- context_cot: bfloat16 [4, 1024, 2048], P('dp', 'seq'), may hold values from -6 to 6
Outputs:
- context: bfloat16 [4, 1024, 2048], P('dp', 'seq')
- query_grad: bfloat16 [4, 1024, 2048], P('dp', 'seq')
- memory_grad: bfloat16 [4, 1024, 1792], P('dp', 'seq')
The draws below stay inside these ranges and needn't reach their ends.
All inputs are finite; a program needn't handle non-finite values.
Results may differ from the reference program's by a relative error of at most 0.035.
The reference program's roundings to bfloat16 on the way count: a program that leaves them out, or rounds other values in their place, can miss the bound.
Values may be sent and summed in bfloat16 or wider, within the bound.
A program may use at most 128 MiB of HBM per device.

```python
import math
import jax
import jax.numpy as jnp
import numpy as np
from jax import lax

HEAD = 128
HEADS = 16
ENC = 896
VOCAB = 64000
BLOCK = 64
HD = 2048
NBR_TOKENS = 128
BLOCKS = 16
LENGTH = 1024
SEQS = 4


def draw_queries(key, part):
    base = jax.random.normal(jax.random.fold_in(key, 11), (SEQS, LENGTH, HEADS * HEAD), jnp.float32)
    base = jnp.clip(base, -4.0, 4.0)
    return base.astype(jnp.bfloat16)


def draw_block_memory(key, part):
    base = jax.random.normal(jax.random.fold_in(key, 21), (SEQS, LENGTH, 2 * ENC), jnp.float32)
    base = jnp.clip(base, -4.0, 4.0)
    return base.astype(jnp.bfloat16)


def with_ends(entries, key, smallest, top_value):
    place = [jax.random.randint(jax.random.fold_in(key, axis), (), 0, length) for axis, length in enumerate(entries.shape)]
    widest = entries.shape.index(max(entries.shape))
    neighbour = place[:widest] + [(place[widest] + 1) % entries.shape[widest]] + place[widest + 1:]
    return entries.at[tuple(place)].set(smallest).at[tuple(neighbour)].set(top_value)


def shard_levels(rng, dims, cuts, least, high):
    loudness, own = 1.0, jax.random.fold_in(rng, 6)
    for position, shards_of in cuts:
        draws = jnp.exp(jax.random.uniform(jax.random.fold_in(own, position), (shards_of,), jnp.float32, least / len(cuts), high / len(cuts)))
        loudness = loudness * jnp.repeat(draws, dims[position] // shards_of).reshape([-1 if axis == position else 1 for axis in range(len(dims))])
    return loudness


def rank_bounds(number_of, lean):
    loads = [(1 << 20) // math.isqrt(standing ** lean) + 1 for standing in range(1, number_of + 1)]
    deviation = 1 + sum(loads) // (1 << 30)
    return np.cumsum(np.array([max(1, weight // deviation) for weight in loads]))


def skewed_ids(stream_key, shape, amount, lean):
    grid = rank_bounds(amount, lean)
    pick = jax.random.randint(jax.random.fold_in(stream_key, 1), shape, 0, int(grid[amount - 1]))
    standing = jnp.searchsorted(jnp.asarray(grid, jnp.int32), pick, side="right")
    return jax.random.permutation(jax.random.fold_in(stream_key, 2), amount)[standing].astype(jnp.int32)


def gaussian(key, dims, scale, limit, pieces=(), dtype=jnp.bfloat16):
    values = jax.random.normal(key, dims, jnp.float32) * scale
    if len(pieces) > 0:
        values = shard_levels(key, dims, pieces, -0.22, 0.18) * values
    return jnp.clip(values, min=-limit, max=limit).astype(dtype)


def setup_inputs(seed: int = 0) -> dict:
    key_of = jax.random.split(jax.random.key(seed), 10)
    queries = draw_queries(jax.random.fold_in(key_of[9], 71), 0)
    block_memory = draw_block_memory(jax.random.fold_in(key_of[9], 71), 0)
    neighbour_ids = with_ends(skewed_ids(key_of[2], (SEQS, BLOCKS, NBR_TOKENS), VOCAB, 2), jax.random.fold_in(key_of[2], 3), 0, VOCAB - 1).astype(jnp.int32)
    embedding = gaussian(key_of[3], (ENC, VOCAB), 1.0, 6.0, ((0, 8),))
    enc_query_w = gaussian(key_of[4], (ENC, ENC), ENC ** -0.5, 0.1875, ((0, 4),))
    enc_out_w = gaussian(key_of[5], (ENC, ENC), ENC ** -0.5, 0.1875, ((0, 4),))
    key_w = gaussian(key_of[6], (ENC, HD), ENC ** -0.5, 0.1875, ((0, 4),))
    value_w = gaussian(key_of[7], (ENC, HD), ENC ** -0.5, 0.1875, ((0, 4),))
    context_cot = gaussian(key_of[8], (SEQS, LENGTH, HD), 1.0, 6.0, ((0, 4), (1, 8)))
    return {"queries": queries, "block_memory": block_memory, "neighbour_ids": neighbour_ids, "embedding": embedding, "enc_query_w": enc_query_w, "enc_out_w": enc_out_w, "key_w": key_w, "value_w": value_w, "context_cot": context_cot}


def softmax_rows(scores):
    top = lax.optimization_barrier(jnp.max(scores, axis=-1, keepdims=True))
    expo = jnp.exp(scores - top)
    return expo / lax.optimization_barrier(jnp.sum(expo, axis=-1, keepdims=True))

def encode(embedded, memory, enc_query_w, enc_out_w):
    count, nbr, width = embedded.shape
    heads = width // HEAD
    flat = embedded.reshape(count * nbr, width)
    enc_queries = jnp.dot(flat, enc_query_w, preferred_element_type=jnp.float32).astype(jnp.bfloat16)
    enc_queries = enc_queries.reshape(count, nbr, heads, HEAD)
    split = memory.reshape(count, BLOCK, 2, heads, HEAD)
    mem_key = split[:, :, 0]
    mem_value = split[:, :, 1]
    scores = jnp.einsum('cnhd,cmhd->chnm', enc_queries.astype(jnp.float32), mem_key.astype(jnp.float32)) * HEAD ** (-0.5)
    enc_probs = softmax_rows(scores)
    enc_weights = enc_probs.astype(jnp.bfloat16)
    attended = jnp.einsum('chnm,cmhd->cnhd', enc_weights.astype(jnp.float32), mem_value.astype(jnp.float32)).astype(jnp.bfloat16)
    mixed = jnp.dot(attended.reshape(count * nbr, width), enc_out_w, preferred_element_type=jnp.float32)
    encoded = (flat.astype(jnp.float32) + mixed).astype(jnp.bfloat16)
    return (encoded, (enc_queries, mem_key, mem_value, enc_probs, enc_weights))

def encode_grad(encoded_grad, saved, enc_out_w):
    enc_queries, mem_key, mem_value, enc_probs, enc_weights = saved
    count, nbr, heads, head = enc_queries.shape
    attended_grad = jnp.dot(encoded_grad, enc_out_w.T, preferred_element_type=jnp.float32).astype(jnp.bfloat16)
    attended_grad = attended_grad.reshape(count, nbr, heads, head).astype(jnp.float32)
    inner = jnp.einsum('cnhd,cmhd->chnm', attended_grad, mem_value.astype(jnp.float32))
    centred = inner - lax.optimization_barrier(jnp.sum(enc_probs * inner, axis=-1, keepdims=True))
    enc_d_scores = (enc_probs * centred * HEAD ** (-0.5)).astype(jnp.bfloat16)
    key_part = jnp.einsum('chnm,cnhd->cmhd', enc_d_scores.astype(jnp.float32), enc_queries.astype(jnp.float32))
    value_part = jnp.einsum('chnm,cnhd->cmhd', enc_weights.astype(jnp.float32), attended_grad)
    both = jnp.stack([key_part, value_part], axis=2)
    return both.reshape(count * BLOCK, 2 * heads * head).astype(jnp.bfloat16)

def attend(group_q, group_k, group_v):
    scores = jnp.einsum('cthd,cnhd->chtn', group_q.astype(jnp.float32), group_k.astype(jnp.float32)) * HEAD ** (-0.5)
    probs = softmax_rows(scores)
    weights = probs.astype(jnp.bfloat16)
    ctx = jnp.einsum('chtn,cnhd->cthd', weights.astype(jnp.float32), group_v.astype(jnp.float32)).astype(jnp.bfloat16)
    return (ctx, probs, weights)

def attend_grad(group_q, group_k, group_v, group_c, probs, weights):
    cot = group_c.astype(jnp.float32)
    d_probs = jnp.einsum('cthd,cnhd->chtn', cot, group_v.astype(jnp.float32))
    centred = d_probs - lax.optimization_barrier(jnp.sum(probs * d_probs, axis=-1, keepdims=True))
    d_scores = (probs * centred * HEAD ** (-0.5)).astype(jnp.bfloat16).astype(jnp.float32)
    d_query = jnp.einsum('chtn,cnhd->cthd', d_scores, group_k.astype(jnp.float32)).astype(jnp.bfloat16)
    d_key = jnp.einsum('chtn,cthd->cnhd', d_scores, group_q.astype(jnp.float32))
    d_value = jnp.einsum('chtn,cthd->cnhd', weights.astype(jnp.float32), cot)
    return (d_query, d_key, d_value)

def sequence(query_rows, memory_rows, ids, cot_rows, embedding, enc_query_w, enc_out_w, key_w, value_w):
    length, width = query_rows.shape
    count = length // BLOCK
    nbr = ids.shape[1]
    heads = width // HEAD
    embedded = jnp.take(embedding, ids.reshape(-1), axis=1).T.reshape(count, nbr, -1)
    encoded, saved = encode(embedded, memory_rows, enc_query_w, enc_out_w)
    keys = jnp.dot(encoded, key_w, preferred_element_type=jnp.float32).astype(jnp.bfloat16).reshape(count, nbr, heads, HEAD)
    values = jnp.dot(encoded, value_w, preferred_element_type=jnp.float32).astype(jnp.bfloat16).reshape(count, nbr, heads, HEAD)
    zero_rows = jnp.zeros((BLOCK - 1, width), jnp.bfloat16)
    group_q = jnp.concatenate([query_rows[BLOCK - 1:], zero_rows], axis=0).reshape(count, BLOCK, heads, HEAD)
    group_c = jnp.concatenate([cot_rows[BLOCK - 1:], zero_rows], axis=0).reshape(count, BLOCK, heads, HEAD)
    ctx, probs, weights = attend(group_q, keys, values)
    d_query, d_key, d_value = attend_grad(group_q, keys, values, group_c, probs, weights)
    context = jnp.concatenate([zero_rows, ctx.reshape(length, width)[:length - BLOCK + 1]], axis=0)
    query_grad = jnp.concatenate([zero_rows, d_query.reshape(length, width)[:length - BLOCK + 1]], axis=0)
    key_b = d_key.astype(jnp.bfloat16).reshape(count * nbr, width)
    value_b = d_value.astype(jnp.bfloat16).reshape(count * nbr, width)
    encoded_grad = (jnp.dot(key_b, key_w.T, preferred_element_type=jnp.float32) + jnp.dot(value_b, value_w.T, preferred_element_type=jnp.float32)).astype(jnp.bfloat16)
    memory_grad = encode_grad(encoded_grad, saved, enc_out_w)
    return (context, query_grad, memory_grad)

def reference(queries, block_memory, neighbour_ids, embedding, enc_query_w, enc_out_w, key_w, value_w, context_cot):

    def one_sequence(items):
        query_rows, memory_rows, ids, cot_rows = items
        return sequence(query_rows, memory_rows, ids, cot_rows, embedding, enc_query_w, enc_out_w, key_w, value_w)
    context, query_grad, memory_grad = lax.map(one_sequence, (queries, block_memory, neighbour_ids, context_cot))
    return (context, query_grad, memory_grad)
```

```python
import functools

import jax
import jax.numpy as jnp
from jax import lax
from jax.experimental import pallas as pl
from jax.experimental.pallas import tpu as pltpu
from jax.sharding import PartitionSpec as P

HEAD = 128
BLOCK = 64
SCALE = HEAD ** (-0.5)
F32 = jnp.float32
BF16 = jnp.bfloat16
MESH = pl.DeviceIdType.MESH


def ids_kernel(seqs, q_ref, c_ref, ids_ref, ids_out, halo_q, halo_c, send, recv, halo_send, halo_recv, local):
    dp = lax.axis_index("dp")
    sq = lax.axis_index("seq")
    own = pltpu.make_async_copy(ids_ref, ids_out.at[sq], local)
    own.start()
    barrier = pltpu.get_barrier_semaphore()
    for k in range(1, seqs):
        pl.semaphore_signal(
            barrier, inc=1, device_id=(dp, lax.rem(sq + k, seqs)), device_id_type=MESH
        )
    pl.semaphore_wait(barrier, seqs - 1)

    copies = []
    for k in range(1, seqs):
        copies.append(
            pltpu.make_async_remote_copy(
                src_ref=ids_ref,
                dst_ref=ids_out.at[sq],
                send_sem=send.at[k],
                recv_sem=recv.at[k],
                device_id=(dp, lax.rem(sq + k, seqs)),
                device_id_type=MESH,
            )
        )
        copies[-1].start()
    for i, (src, dst) in enumerate(((q_ref, halo_q), (c_ref, halo_c))):
        copies.append(
            pltpu.make_async_remote_copy(
                src_ref=src.at[pl.ds(0, BLOCK)],
                dst_ref=dst,
                send_sem=halo_send.at[i],
                recv_sem=halo_recv.at[i],
                device_id=(dp, lax.rem(sq + seqs - 1, seqs)),
                device_id_type=MESH,
            )
        )
        copies[-1].start()
    own.wait()
    for copy in copies:
        copy.wait()


def share_ids(q, c, ids):
    seqs = lax.axis_size("seq")
    anywhere = pl.BlockSpec(memory_space=pl.ANY)
    dma = pltpu.SemaphoreType.DMA
    shape = jax.ShapeDtypeStruct
    return pl.pallas_call(
        functools.partial(ids_kernel, seqs),
        out_shape=[
            shape((seqs,) + ids.shape, jnp.int32),
            shape((BLOCK, q.shape[1]), BF16),
            shape((BLOCK, q.shape[1]), BF16),
        ],
        in_specs=[anywhere] * 3,
        out_specs=[anywhere] * 3,
        scratch_shapes=[dma((seqs,)), dma((seqs,)), dma((2,)), dma((2,)), dma],
        compiler_params=pltpu.CompilerParams(collective_id=1, has_side_effects=True),
    )(q, c, ids)


def look_kernel(ids, table, out):
    seqs, count, nbr = ids.shape
    feats = table.shape[0]
    lane = lax.broadcasted_iota(jnp.int32, (feats, HEAD), 1)
    step = 8

    def chunk(to, carry):
        for b in range(count):
            for part in range(nbr // HEAD):

                def some(i, acc):
                    for t in range(step):
                        j = i * step + t
                        token = ids[to, b, part * HEAD + j]
                        start = pl.multiple_of((token >> 7) << 7, HEAD)
                        tile = table[:, pl.ds(start, HEAD)].astype(F32)
                        moved = pltpu.roll(tile, (j - token) & (HEAD - 1), 1)
                        acc = jnp.where(lane == j, moved, acc)
                    return acc

                acc = lax.fori_loop(0, HEAD // step, some, jnp.zeros((feats, HEAD), F32))
                first = b * nbr + part * HEAD
                out[to, :, first : first + HEAD] = acc.astype(BF16)
        return carry

    lax.fori_loop(0, seqs, chunk, 0)


def look_up(ids, table):
    seqs, count, nbr = ids.shape
    feats = table.shape[0]
    return pl.pallas_call(
        look_kernel,
        out_shape=jax.ShapeDtypeStruct((seqs, feats, count * nbr), BF16),
        in_specs=[
            pl.BlockSpec(memory_space=pltpu.SMEM),
            pl.BlockSpec(memory_space=pltpu.VMEM),
        ],
        out_specs=pl.BlockSpec(memory_space=pltpu.VMEM),
    )(ids, table)


def gather_kernel(
    dps,
    seqs,
    stage,
    eq_ref,
    eo_ref,
    kw_ref,
    vw_ref,
    emb_out,
    eq_out,
    eo_out,
    kw_out,
    vw_out,
    w_send,
    w_recv,
    fwd_send,
    emb_send,
    emb_recv,
    local,
):
    dp = lax.axis_index("dp")
    sq = lax.axis_index("seq")
    core = lax.rem(sq, 2)
    mate = sq + 1 - 2 * core
    weights = ((eq_ref, eq_out), (eo_ref, eo_out), (kw_ref, kw_out), (vw_ref, vw_out))
    own = [pltpu.make_async_copy(stage.at[sq], emb_out.at[sq], local.at[4])]
    for w, (src, dst) in enumerate(weights):
        own.append(pltpu.make_async_copy(src, dst.at[dp], local.at[w]))
    for copy in own:
        copy.start()

    barrier = pltpu.get_barrier_semaphore()
    for k in range(1, seqs):
        pl.semaphore_signal(
            barrier, inc=1, device_id=(dp, lax.rem(sq + k, seqs)), device_id_type=MESH
        )
    for k in range(1, dps):
        pl.semaphore_signal(
            barrier, inc=1, device_id=(lax.rem(dp + k, dps), sq), device_id_type=MESH
        )
    pl.semaphore_wait(barrier, seqs - 1 + dps - 1)

    def w_copy(w, to):
        src, dst = weights[w]
        return pltpu.make_async_remote_copy(
            src_ref=src,
            dst_ref=dst.at[dp],
            send_sem=w_send.at[w, to],
            recv_sem=w_recv.at[w, dp],
            device_id=(to, sq),
            device_id_type=MESH,
        )

    def w_forward(w, owner):
        dst = weights[w][1]
        return pltpu.make_async_remote_copy(
            src_ref=dst.at[owner],
            dst_ref=dst.at[owner],
            send_sem=fwd_send.at[w, owner],
            recv_sem=w_recv.at[w, owner],
            device_id=(dp, mate),
            device_id_type=MESH,
        )

    def emb_copy(to):
        return pltpu.make_async_remote_copy(
            src_ref=stage.at[to],
            dst_ref=emb_out.at[sq],
            send_sem=emb_send.at[to],
            recv_sem=emb_recv.at[sq],
            device_id=(dp, to),
            device_id_type=MESH,
        )

    def arrived(ref, sem):
        pltpu.make_async_copy(ref, ref, sem).wait()

    for side in range(2):

        @pl.when(core == side)
        def _():
            for w in (side, 2 + side):
                for k in range(1, dps):
                    w_copy(w, lax.rem(dp + k, dps)).start()

    for k in range(1, seqs):
        emb_copy(lax.rem(sq + k, seqs)).start()

    for side in range(2):

        @pl.when(core == side)
        def _():
            for w in (side, 2 + side):
                for k in range(1, dps):
                    owner = lax.rem(dp + k, dps)
                    arrived(weights[w][1].at[owner], w_recv.at[w, owner])
                    w_forward(w, owner).start()
            for w in (1 - side, 3 - side):
                for k in range(1, dps):
                    owner = lax.rem(dp + k, dps)
                    arrived(weights[w][1].at[owner], w_recv.at[w, owner])
            for w in (side, 2 + side):
                for k in range(1, dps):
                    w_copy(w, lax.rem(dp + k, dps)).wait_send()
                    w_forward(w, lax.rem(dp + k, dps)).wait_send()

    for copy in own:
        copy.wait()
    for k in range(1, seqs):
        other = lax.rem(sq + k, seqs)
        emb_copy(other).wait_send()
        arrived(emb_out.at[other], emb_recv.at[other])


def gather_all(stage, eq, eo, kw, vw):
    dps, seqs = lax.axis_size("dp"), lax.axis_size("seq")
    anywhere = pl.BlockSpec(memory_space=pl.ANY)
    dma = pltpu.SemaphoreType.DMA
    shape = jax.ShapeDtypeStruct
    return pl.pallas_call(
        functools.partial(gather_kernel, dps, seqs),
        out_shape=[shape(stage.shape, BF16)]
        + [shape((dps,) + w.shape, BF16) for w in (eq, eo, kw, vw)],
        in_specs=[anywhere] * 5,
        out_specs=[anywhere] * 5,
        scratch_shapes=[
            dma((4, dps)),
            dma((4, dps)),
            dma((4, dps)),
            dma((seqs,)),
            dma((seqs,)),
            dma((5,)),
        ],
        compiler_params=pltpu.CompilerParams(collective_id=0, has_side_effects=True),
    )(stage, eq, eo, kw, vw)


def nt(a, b):
    return lax.dot_general(a, b, (((1,), (1,)), ((), ())), preferred_element_type=F32)


def nn(a, b):
    return lax.dot_general(a, b, (((1,), (0,)), ((), ())), preferred_element_type=F32)


def tn(a, b):
    return lax.dot_general(a, b, (((0,), (0,)), ((), ())), preferred_element_type=F32)


def softmax_rows(scores):
    top = jnp.max(scores, axis=-1, keepdims=True)
    expo = jnp.exp(scores - top)
    return expo / jnp.sum(expo, axis=-1, keepdims=True)


def math_kernel(
    nbr,
    embt,
    mem,
    gq,
    gc,
    eqw,
    eow,
    kw,
    vw,
    ctx_out,
    grad_out,
    mem_out,
    emb,
    eq,
    att,
    probs_buf,
    keys,
    values,
    dkeys,
    dvalues,
):
    count = mem.shape[0] // BLOCK
    width = eqw.shape[0]
    enc_heads = width // HEAD
    heads = kw.shape[1] // HEAD
    emb[...] = embt[...].T
    eq[...] = nn(emb[...], eqw[...]).astype(BF16)
    for h in range(enc_heads):
        cols = slice(h * HEAD, (h + 1) * HEAD)
        vcols = slice(width + h * HEAD, width + (h + 1) * HEAD)
        for b in range(count):
            rows = slice(b * nbr, (b + 1) * nbr)
            toks = slice(b * BLOCK, (b + 1) * BLOCK)
            probs = softmax_rows(nt(eq[rows, cols], mem[toks, cols]) * SCALE)
            probs_buf[h * count + b] = probs
            att[rows, cols] = nn(probs.astype(BF16), mem[toks, vcols]).astype(BF16)
    encoded = (emb[...].astype(F32) + nn(att[...], eow[...])).astype(BF16)
    keys[...] = nn(encoded, kw[...]).astype(BF16)
    values[...] = nn(encoded, vw[...]).astype(BF16)

    def head(h, carry):
        cols = pl.ds(pl.multiple_of(h * HEAD, HEAD), HEAD)
        for b in range(count):
            rows = slice(b * nbr, (b + 1) * nbr)
            toks = slice(b * BLOCK, (b + 1) * BLOCK)
            q, g, k, v = gq[toks, cols], gc[toks, cols], keys[rows, cols], values[rows, cols]
            probs = softmax_rows(nt(q, k) * SCALE)
            weights = probs.astype(BF16)
            ctx_out[toks, cols] = nn(weights, v).astype(BF16)
            d_probs = nt(g, v)
            centred = d_probs - jnp.sum(probs * d_probs, axis=-1, keepdims=True)
            d_scores = (probs * centred * SCALE).astype(BF16)
            grad_out[toks, cols] = nn(d_scores, k).astype(BF16)
            dkeys[rows, cols] = tn(d_scores, q).astype(BF16)
            dvalues[rows, cols] = tn(weights, g).astype(BF16)
        return carry

    lax.fori_loop(0, heads, head, 0, unroll=4)
    enc_grad = (nt(dkeys[...], kw[...]) + nt(dvalues[...], vw[...])).astype(BF16)
    att[...] = nt(enc_grad, eow[...]).astype(BF16)
    for h in range(enc_heads):
        cols = slice(h * HEAD, (h + 1) * HEAD)
        vcols = slice(width + h * HEAD, width + (h + 1) * HEAD)
        for b in range(count):
            rows = slice(b * nbr, (b + 1) * nbr)
            toks = slice(b * BLOCK, (b + 1) * BLOCK)
            probs = probs_buf[h * count + b]
            grad = att[rows, cols]
            inner = nt(grad, mem[toks, vcols])
            centred = inner - jnp.sum(probs * inner, axis=-1, keepdims=True)
            d_scores = (probs * centred * SCALE).astype(BF16)
            mem_out[toks, cols] = tn(d_scores, eq[rows, cols]).astype(BF16)
            mem_out[toks, vcols] = tn(probs.astype(BF16), grad).astype(BF16)


def math_all(nbr, embt, mem, gq, gc, eqw, eow, kw, vw):
    width, tokens = embt.shape
    count = mem.shape[0] // BLOCK
    wide = kw.shape[1]
    vmem = pl.BlockSpec(memory_space=pltpu.VMEM)
    shape = jax.ShapeDtypeStruct
    return pl.pallas_call(
        functools.partial(math_kernel, nbr),
        out_shape=[shape(gq.shape, BF16), shape(gq.shape, BF16), shape(mem.shape, BF16)],
        in_specs=[vmem] * 8,
        out_specs=[vmem] * 3,
        scratch_shapes=[
            pltpu.VMEM((tokens, width), BF16),
            pltpu.VMEM((tokens, width), BF16),
            pltpu.VMEM((tokens, width), BF16),
            pltpu.VMEM((width // HEAD * count, nbr, BLOCK), F32),
        ]
        + [pltpu.VMEM((tokens, wide), BF16)] * 4,
    )(embt, mem, gq, gc, eqw, eow, kw, vw)


def body(
    queries,
    block_memory,
    neighbour_ids,
    embedding,
    enc_query_w,
    enc_out_w,
    key_w,
    value_w,
    context_cot,
):
    q, mem, ids, cot = queries[0], block_memory[0], neighbour_ids[0], context_cot[0]
    tokens, wide = q.shape
    nbr = ids.shape[1]
    seqs = lax.axis_size("seq")
    all_ids, halo_q, halo_c = share_ids(q, cot, ids)
    stage = look_up(all_ids, embedding)
    emb, *gathered = gather_all(stage, enc_query_w, enc_out_w, key_w, value_w)
    flat = [w.reshape(-1, w.shape[2]) for w in gathered]
    last = lax.axis_index("seq") == seqs - 1
    halo_q = jnp.where(last, jnp.zeros_like(halo_q), halo_q)
    halo_c = jnp.where(last, jnp.zeros_like(halo_c), halo_c)
    gq = jnp.concatenate([q[BLOCK - 1 :], halo_q[: BLOCK - 1]], axis=0)
    gc = jnp.concatenate([cot[BLOCK - 1 :], halo_c[: BLOCK - 1]], axis=0)
    ctx, grad, mem_grad = math_all(nbr, emb.reshape(-1, emb.shape[2]), mem, gq, gc, *flat)
    ring = [(s, s + 1) for s in range(seqs - 1)]
    back_c = lax.ppermute(ctx[tokens - BLOCK :], "seq", ring)
    back_q = lax.ppermute(grad[tokens - BLOCK :], "seq", ring)
    context = jnp.concatenate([back_c[1:], ctx[: tokens - BLOCK + 1]], axis=0)
    query_grad = jnp.concatenate([back_q[1:], grad[: tokens - BLOCK + 1]], axis=0)
    return (context[None], query_grad[None], mem_grad[None])


def solution(mesh):
    rows = P("dp", "seq", None)
    split = P("dp", None)
    return jax.shard_map(
        body,
        mesh=mesh,
        in_specs=(rows, rows, rows, P("seq", None), split, split, split, split, rows),
        out_specs=(rows, rows, rows),
        check_vma=False,
    )
```

```python
import functools

import jax
import jax.numpy as jnp
from jax import lax
from jax.experimental import pallas as pl
from jax.experimental.pallas import tpu as pltpu
from jax.sharding import PartitionSpec as P

HEAD = 128
BLOCK = 64
SCALE = HEAD ** (-0.5)
F32 = jnp.float32
BF16 = jnp.bfloat16
MESH = pl.DeviceIdType.MESH


def ids_kernel(seqs, q_ref, c_ref, ids_ref, ids_out, halo_q, halo_c, send, recv, halo_send, halo_recv, local):
    dp = lax.axis_index("dp")
    sq = lax.axis_index("seq")
    own = pltpu.make_async_copy(ids_ref, ids_out.at[sq], local)
    own.start()
    barrier = pltpu.get_barrier_semaphore()
    for k in range(1, seqs):
        pl.semaphore_signal(
            barrier, inc=1, device_id=(dp, lax.rem(sq + k, seqs)), device_id_type=MESH
        )
    pl.semaphore_wait(barrier, seqs - 1)

    copies = []
    for k in range(1, seqs):
        copies.append(
            pltpu.make_async_remote_copy(
                src_ref=ids_ref,
                dst_ref=ids_out.at[sq],
                send_sem=send.at[k],
                recv_sem=recv.at[k],
                device_id=(dp, lax.rem(sq + k, seqs)),
                device_id_type=MESH,
            )
        )
        copies[-1].start()
    for i, (src, dst) in enumerate(((q_ref, halo_q), (c_ref, halo_c))):
        copies.append(
            pltpu.make_async_remote_copy(
                src_ref=src.at[pl.ds(0, BLOCK)],
                dst_ref=dst,
                send_sem=halo_send.at[i],
                recv_sem=halo_recv.at[i],
                device_id=(dp, lax.rem(sq + seqs - 1, seqs)),
                device_id_type=MESH,
            )
        )
        copies[-1].start()
    own.wait()
    for copy in copies:
        copy.wait()


def share_ids(q, c, ids):
    seqs = lax.axis_size("seq")
    anywhere = pl.BlockSpec(memory_space=pl.ANY)
    dma = pltpu.SemaphoreType.DMA
    shape = jax.ShapeDtypeStruct
    return pl.pallas_call(
        functools.partial(ids_kernel, seqs),
        out_shape=[
            shape((seqs,) + ids.shape, jnp.int32),
            shape((BLOCK, q.shape[1]), BF16),
            shape((BLOCK, q.shape[1]), BF16),
        ],
        in_specs=[anywhere] * 3,
        out_specs=[anywhere] * 3,
        scratch_shapes=[dma((seqs,)), dma((seqs,)), dma((2,)), dma((2,)), dma],
        compiler_params=pltpu.CompilerParams(collective_id=1, has_side_effects=True),
    )(q, c, ids)


def look_kernel(ids, table, out):
    seqs, count, nbr = ids.shape
    feats = table.shape[0]
    lane = lax.broadcasted_iota(jnp.int32, (feats, HEAD), 1)
    step = 32

    def chunk(to, carry):
        for b in range(count):
            for part in range(nbr // HEAD):

                def some(i, acc):
                    for t in range(step):
                        j = i * step + t
                        token = ids[to, b, part * HEAD + j]
                        start = pl.multiple_of((token >> 7) << 7, HEAD)
                        tile = table[:, pl.ds(start, HEAD)].astype(F32)
                        moved = pltpu.roll(tile, (j - token) & (HEAD - 1), 1)
                        acc = jnp.where(lane == j, moved, acc)
                    return acc

                acc = lax.fori_loop(0, HEAD // step, some, jnp.zeros((feats, HEAD), F32))
                first = b * nbr + part * HEAD
                out[to, :, first : first + HEAD] = acc.astype(BF16)
        return carry

    lax.fori_loop(0, seqs, chunk, 0)


def look_up(ids, table):
    seqs, count, nbr = ids.shape
    feats = table.shape[0]
    return pl.pallas_call(
        look_kernel,
        out_shape=jax.ShapeDtypeStruct((seqs, feats, count * nbr), BF16),
        in_specs=[
            pl.BlockSpec(memory_space=pltpu.SMEM),
            pl.BlockSpec(memory_space=pltpu.VMEM),
        ],
        out_specs=pl.BlockSpec(memory_space=pltpu.VMEM),
    )(ids, table)


def swap_kernel(seqs, stage, emb_out, send, recv, local):
    dp = lax.axis_index("dp")
    sq = lax.axis_index("seq")
    own = pltpu.make_async_copy(stage.at[sq], emb_out.at[sq], local)
    own.start()
    barrier = pltpu.get_barrier_semaphore()
    for k in range(1, seqs):
        pl.semaphore_signal(
            barrier, inc=1, device_id=(dp, lax.rem(sq + k, seqs)), device_id_type=MESH
        )
    pl.semaphore_wait(barrier, seqs - 1)
    copies = []
    for k in range(1, seqs):
        to = lax.rem(sq + k, seqs)
        copies.append(
            pltpu.make_async_remote_copy(
                src_ref=stage.at[to],
                dst_ref=emb_out.at[sq],
                send_sem=send.at[k],
                recv_sem=recv.at[k],
                device_id=(dp, to),
                device_id_type=MESH,
            )
        )
        copies[-1].start()
    own.wait()
    for copy in copies:
        copy.wait()


def swap_features(stage):
    seqs = lax.axis_size("seq")
    anywhere = pl.BlockSpec(memory_space=pl.ANY)
    dma = pltpu.SemaphoreType.DMA
    return pl.pallas_call(
        functools.partial(swap_kernel, seqs),
        out_shape=jax.ShapeDtypeStruct(stage.shape, BF16),
        in_specs=[anywhere],
        out_specs=anywhere,
        scratch_shapes=[dma((seqs,)), dma((seqs,)), dma],
        compiler_params=pltpu.CompilerParams(collective_id=0, has_side_effects=True),
    )(stage)


def spread(pair):
    dps, seqs = lax.axis_size("dp"), lax.axis_size("seq")
    mine = jnp.where(lax.axis_index("seq") % 2 == 0, pair[0], pair[1])
    fetched = [
        lax.ppermute(mine, "dp", [(s, (s + k) % dps) for s in range(dps)]) for k in range(1, dps)
    ]
    passed = [lax.ppermute(f, "seq", [(s, s ^ 1) for s in range(seqs)]) for f in fetched]
    return list(pair) + fetched + passed


def nt(a, b):
    return lax.dot_general(a, b, (((1,), (1,)), ((), ())), preferred_element_type=F32)


def nn(a, b):
    return lax.dot_general(a, b, (((1,), (0,)), ((), ())), preferred_element_type=F32)


def tn(a, b):
    return lax.dot_general(a, b, (((0,), (0,)), ((), ())), preferred_element_type=F32)


def softmax_rows(scores):
    top = jnp.max(scores, axis=-1, keepdims=True)
    expo = jnp.exp(scores - top)
    return expo / jnp.sum(expo, axis=-1, keepdims=True)


def math_kernel(nbr, dps, embt, mem, gq, gc, *refs):
    pieces = 2 * dps
    enc_refs, wide_refs = refs[:pieces], refs[pieces : 2 * pieces]
    math_inner(nbr, dps, enc_refs, wide_refs, embt, mem, gq, gc, *refs[2 * pieces :])


def math_inner(
    nbr,
    dps,
    enc_refs,
    wide_refs,
    embt,
    mem,
    gq,
    gc,
    ctx_out,
    grad_out,
    mem_out,
    eqw,
    eow,
    kw,
    vw,
    sems,
    emb,
    eq,
    att,
    probs_buf,
    keys,
    values,
    dkeys,
    dvalues,
):
    count = mem.shape[0] // BLOCK
    width = eqw.shape[0]
    enc_heads = width // HEAD
    heads = kw.shape[1] // HEAD
    dp = lax.axis_index("dp")
    core = lax.rem(lax.axis_index("seq"), 2)

    def loads(refs, pair, base, side):
        piece = refs[0].shape[0]
        copies = []
        for i, ref in enumerate(refs):
            if i < 2:
                target, owner = pair[i], dp
            elif i < dps + 1:
                target, owner = pair[side], lax.rem(dp - (i - 1) + dps, dps)
            else:
                target, owner = pair[1 - side], lax.rem(dp - (i - dps) + dps, dps)
            rows = pl.ds(pl.multiple_of(owner * piece, 8), piece)
            copies.append(pltpu.make_async_copy(ref, target.at[rows], sems.at[base + i]))
        return copies

    for side in range(2):

        @pl.when(core == side)
        def _():
            for copy in loads(enc_refs, (eqw, eow), 0, side):
                copy.start()
            for copy in loads(wide_refs, (kw, vw), 2 * dps, side):
                copy.start()

    emb[...] = embt[...].T
    for copy in loads(enc_refs, (eqw, eow), 0, 0):
        copy.wait()
    eq[...] = nn(emb[...], eqw[...]).astype(BF16)
    for h in range(enc_heads):
        cols = slice(h * HEAD, (h + 1) * HEAD)
        vcols = slice(width + h * HEAD, width + (h + 1) * HEAD)
        for b in range(count):
            rows = slice(b * nbr, (b + 1) * nbr)
            toks = slice(b * BLOCK, (b + 1) * BLOCK)
            probs = softmax_rows(nt(eq[rows, cols], mem[toks, cols]) * SCALE)
            probs_buf[h * count + b] = probs
            att[rows, cols] = nn(probs.astype(BF16), mem[toks, vcols]).astype(BF16)
    encoded = (emb[...].astype(F32) + nn(att[...], eow[...])).astype(BF16)
    for copy in loads(wide_refs, (kw, vw), 2 * dps, 0):
        copy.wait()
    keys[...] = nn(encoded, kw[...]).astype(BF16)
    values[...] = nn(encoded, vw[...]).astype(BF16)

    def head(h, carry):
        cols = pl.ds(pl.multiple_of(h * HEAD, HEAD), HEAD)
        for b in range(count):
            rows = slice(b * nbr, (b + 1) * nbr)
            toks = slice(b * BLOCK, (b + 1) * BLOCK)
            q, g, k, v = gq[toks, cols], gc[toks, cols], keys[rows, cols], values[rows, cols]
            probs = softmax_rows(nt(q, k) * SCALE)
            weights = probs.astype(BF16)
            ctx_out[toks, cols] = nn(weights, v).astype(BF16)
            d_probs = nt(g, v)
            centred = d_probs - jnp.sum(probs * d_probs, axis=-1, keepdims=True)
            d_scores = (probs * centred * SCALE).astype(BF16)
            grad_out[toks, cols] = nn(d_scores, k).astype(BF16)
            dkeys[rows, cols] = tn(d_scores, q).astype(BF16)
            dvalues[rows, cols] = tn(weights, g).astype(BF16)
        return carry

    lax.fori_loop(0, heads, head, 0, unroll=4)
    enc_grad = (nt(dkeys[...], kw[...]) + nt(dvalues[...], vw[...])).astype(BF16)
    att[...] = nt(enc_grad, eow[...]).astype(BF16)
    for h in range(enc_heads):
        cols = slice(h * HEAD, (h + 1) * HEAD)
        vcols = slice(width + h * HEAD, width + (h + 1) * HEAD)
        for b in range(count):
            rows = slice(b * nbr, (b + 1) * nbr)
            toks = slice(b * BLOCK, (b + 1) * BLOCK)
            probs = probs_buf[h * count + b]
            grad = att[rows, cols]
            inner = nt(grad, mem[toks, vcols])
            centred = inner - jnp.sum(probs * inner, axis=-1, keepdims=True)
            d_scores = (probs * centred * SCALE).astype(BF16)
            mem_out[toks, cols] = tn(d_scores, eq[rows, cols]).astype(BF16)
            mem_out[toks, vcols] = tn(probs.astype(BF16), grad).astype(BF16)


def math_all(nbr, embt, mem, gq, gc, enc, wides):
    width, tokens = embt.shape
    count = mem.shape[0] // BLOCK
    wide = gq.shape[1]
    dps = lax.axis_size("dp")
    anywhere = pl.BlockSpec(memory_space=pl.ANY)
    vmem = pl.BlockSpec(memory_space=pltpu.VMEM)
    shape = jax.ShapeDtypeStruct
    return pl.pallas_call(
        functools.partial(math_kernel, nbr, dps),
        out_shape=[shape(gq.shape, BF16), shape(gq.shape, BF16), shape(mem.shape, BF16)],
        in_specs=[vmem] * 4 + [anywhere] * (4 * dps),
        out_specs=[vmem] * 3,
        scratch_shapes=[
            pltpu.VMEM((width, width), BF16),
            pltpu.VMEM((width, width), BF16),
            pltpu.VMEM((width, wide), BF16),
            pltpu.VMEM((width, wide), BF16),
            pltpu.SemaphoreType.DMA((4 * dps,)),
            pltpu.VMEM((tokens, width), BF16),
            pltpu.VMEM((tokens, width), BF16),
            pltpu.VMEM((tokens, width), BF16),
            pltpu.VMEM((width // HEAD * count, nbr, BLOCK), F32),
        ]
        + [pltpu.VMEM((tokens, wide), BF16)] * 4,
    )(embt, mem, gq, gc, *enc, *wides)


def body(
    queries,
    block_memory,
    neighbour_ids,
    embedding,
    enc_query_w,
    enc_out_w,
    key_w,
    value_w,
    context_cot,
):
    q, mem, ids, cot = queries[0], block_memory[0], neighbour_ids[0], context_cot[0]
    tokens, wide = q.shape
    nbr = ids.shape[1]
    seqs = lax.axis_size("seq")
    enc = spread((enc_query_w, enc_out_w))
    wides = spread((key_w, value_w))
    all_ids, halo_q, halo_c = share_ids(q, cot, ids)
    stage = look_up(all_ids, embedding)
    emb = swap_features(stage)
    last = lax.axis_index("seq") == seqs - 1
    halo_q = jnp.where(last, jnp.zeros_like(halo_q), halo_q)
    halo_c = jnp.where(last, jnp.zeros_like(halo_c), halo_c)
    gq = jnp.concatenate([q[BLOCK - 1 :], halo_q[: BLOCK - 1]], axis=0)
    gc = jnp.concatenate([cot[BLOCK - 1 :], halo_c[: BLOCK - 1]], axis=0)
    ctx, grad, mem_grad = math_all(nbr, emb.reshape(-1, emb.shape[2]), mem, gq, gc, enc, wides)
    ring = [(s, s + 1) for s in range(seqs - 1)]
    back_c = lax.ppermute(ctx[tokens - BLOCK :], "seq", ring)
    back_q = lax.ppermute(grad[tokens - BLOCK :], "seq", ring)
    context = jnp.concatenate([back_c[1:], ctx[: tokens - BLOCK + 1]], axis=0)
    query_grad = jnp.concatenate([back_q[1:], grad[: tokens - BLOCK + 1]], axis=0)
    return (context[None], query_grad[None], mem_grad[None])


def solution(mesh):
    rows = P("dp", "seq", None)
    split = P("dp", None)
    return jax.shard_map(
        body,
        mesh=mesh,
        in_specs=(rows, rows, rows, P("seq", None), split, split, split, split, rows),
        out_specs=(rows, rows, rows),
        check_vma=False,
    )
```

```python
import functools

import jax
import jax.numpy as jnp
from jax import lax
from jax.experimental import pallas as pl
from jax.experimental.pallas import tpu as pltpu
from jax.sharding import PartitionSpec as P

HEAD = 128
BLOCK = 64
SCALE = HEAD ** (-0.5)
F32 = jnp.float32
BF16 = jnp.bfloat16
MESH = pl.DeviceIdType.MESH


def ids_kernel(seqs, ids_ref, ids_out, send, recv, local):
    dp = lax.axis_index("dp")
    sq = lax.axis_index("seq")
    own = pltpu.make_async_copy(ids_ref, ids_out.at[sq], local)
    own.start()
    barrier = pltpu.get_barrier_semaphore()
    for k in range(1, seqs):
        pl.semaphore_signal(
            barrier, inc=1, device_id=(dp, lax.rem(sq + k, seqs)), device_id_type=MESH
        )
    pl.semaphore_wait(barrier, seqs - 1)

    copies = []
    for k in range(1, seqs):
        copies.append(
            pltpu.make_async_remote_copy(
                src_ref=ids_ref,
                dst_ref=ids_out.at[sq],
                send_sem=send.at[k],
                recv_sem=recv.at[k],
                device_id=(dp, lax.rem(sq + k, seqs)),
                device_id_type=MESH,
            )
        )
        copies[-1].start()
    own.wait()
    for copy in copies:
        copy.wait()


def share_ids(ids):
    seqs = lax.axis_size("seq")
    anywhere = pl.BlockSpec(memory_space=pl.ANY)
    dma = pltpu.SemaphoreType.DMA
    return pl.pallas_call(
        functools.partial(ids_kernel, seqs),
        out_shape=jax.ShapeDtypeStruct((seqs,) + ids.shape, jnp.int32),
        in_specs=[anywhere],
        out_specs=anywhere,
        scratch_shapes=[dma((seqs,)), dma((seqs,)), dma],
        compiler_params=pltpu.CompilerParams(collective_id=1, has_side_effects=True),
    )(ids)


def look_kernel(ids, table, out):
    seqs, count, nbr = ids.shape
    feats = table.shape[0]
    lane = lax.broadcasted_iota(jnp.int32, (feats, HEAD), 1)
    step = 32

    def chunk(to, carry):
        for b in range(count):
            for part in range(nbr // HEAD):

                def some(i, acc):
                    for t in range(step):
                        j = i * step + t
                        token = ids[to, b, part * HEAD + j]
                        start = pl.multiple_of((token >> 7) << 7, HEAD)
                        tile = table[:, pl.ds(start, HEAD)].astype(F32)
                        moved = pltpu.roll(tile, (j - token) & (HEAD - 1), 1)
                        acc = jnp.where(lane == j, moved, acc)
                    return acc

                acc = lax.fori_loop(0, HEAD // step, some, jnp.zeros((feats, HEAD), F32))
                first = b * nbr + part * HEAD
                out[to, :, first : first + HEAD] = acc.astype(BF16)
        return carry

    lax.fori_loop(0, seqs, chunk, 0)


def look_up(ids, table):
    seqs, count, nbr = ids.shape
    feats = table.shape[0]
    return pl.pallas_call(
        look_kernel,
        out_shape=jax.ShapeDtypeStruct((seqs, feats, count * nbr), BF16),
        in_specs=[
            pl.BlockSpec(memory_space=pltpu.SMEM),
            pl.BlockSpec(memory_space=pltpu.VMEM),
        ],
        out_specs=pl.BlockSpec(memory_space=pltpu.VMEM),
    )(ids, table)


def swap_kernel(seqs, stage, emb_out, send, recv, local):
    dp = lax.axis_index("dp")
    sq = lax.axis_index("seq")
    own = pltpu.make_async_copy(stage.at[sq], emb_out.at[sq], local)
    own.start()
    barrier = pltpu.get_barrier_semaphore()
    for k in range(1, seqs):
        pl.semaphore_signal(
            barrier, inc=1, device_id=(dp, lax.rem(sq + k, seqs)), device_id_type=MESH
        )
    pl.semaphore_wait(barrier, seqs - 1)
    copies = []
    for k in range(1, seqs):
        to = lax.rem(sq + k, seqs)
        copies.append(
            pltpu.make_async_remote_copy(
                src_ref=stage.at[to],
                dst_ref=emb_out.at[sq],
                send_sem=send.at[k],
                recv_sem=recv.at[k],
                device_id=(dp, to),
                device_id_type=MESH,
            )
        )
        copies[-1].start()
    own.wait()
    for copy in copies:
        copy.wait()


def swap_features(stage):
    seqs = lax.axis_size("seq")
    anywhere = pl.BlockSpec(memory_space=pl.ANY)
    dma = pltpu.SemaphoreType.DMA
    return pl.pallas_call(
        functools.partial(swap_kernel, seqs),
        out_shape=jax.ShapeDtypeStruct(stage.shape, BF16),
        in_specs=[anywhere],
        out_specs=anywhere,
        scratch_shapes=[dma((seqs,)), dma((seqs,)), dma],
        compiler_params=pltpu.CompilerParams(collective_id=0, has_side_effects=True),
    )(stage)


def spread(pair):
    dps, seqs = lax.axis_size("dp"), lax.axis_size("seq")
    mine = jnp.where(lax.axis_index("seq") % 2 == 0, pair[0], pair[1])
    fetched = [
        lax.ppermute(mine, "dp", [(s, (s + k) % dps) for s in range(dps)]) for k in range(1, dps)
    ]
    passed = [lax.ppermute(f, "seq", [(s, s ^ 1) for s in range(seqs)]) for f in fetched]
    return list(pair) + fetched + passed


def nt(a, b):
    return lax.dot_general(a, b, (((1,), (1,)), ((), ())), preferred_element_type=F32)


def nn(a, b):
    return lax.dot_general(a, b, (((1,), (0,)), ((), ())), preferred_element_type=F32)


def tn(a, b):
    return lax.dot_general(a, b, (((0,), (0,)), ((), ())), preferred_element_type=F32)


def softmax_rows(scores):
    top = jnp.max(scores, axis=-1, keepdims=True)
    expo = jnp.exp(scores - top)
    return expo / jnp.sum(expo, axis=-1, keepdims=True)


def math_kernel(nbr, dps, embt, mem, rq, rc, halo, *refs):
    pieces = 2 * dps
    enc_refs, wide_refs = refs[:pieces], refs[pieces : 2 * pieces]
    math_inner(nbr, dps, enc_refs, wide_refs, embt, mem, rq, rc, halo, *refs[2 * pieces :])


def math_inner(
    nbr,
    dps,
    enc_refs,
    wide_refs,
    embt,
    mem,
    rq,
    rc,
    halo,
    ctx_out,
    grad_out,
    back_out,
    mem_out,
    eqw,
    eow,
    kw,
    vw,
    sems,
    emb,
    eq,
    att,
    probs_buf,
    keys,
    values,
    dkeys,
    dvalues,
):
    count = mem.shape[0] // BLOCK
    width = eqw.shape[0]
    enc_heads = width // HEAD
    heads = kw.shape[1] // HEAD
    dp = lax.axis_index("dp")
    core = lax.rem(lax.axis_index("seq"), 2)

    def loads(refs, pair, base, side):
        piece = refs[0].shape[0]
        copies = []
        for i, ref in enumerate(refs):
            if i < 2:
                target, owner = pair[i], dp
            elif i < dps + 1:
                target, owner = pair[side], lax.rem(dp - (i - 1) + dps, dps)
            else:
                target, owner = pair[1 - side], lax.rem(dp - (i - dps) + dps, dps)
            rows = pl.ds(pl.multiple_of(owner * piece, 8), piece)
            copies.append(pltpu.make_async_copy(ref, target.at[rows], sems.at[base + i]))
        return copies

    for side in range(2):

        @pl.when(core == side)
        def _():
            for copy in loads(enc_refs, (eqw, eow), 0, side):
                copy.start()
            for copy in loads(wide_refs, (kw, vw), 2 * dps, side):
                copy.start()

    emb[...] = embt[...].T
    for copy in loads(enc_refs, (eqw, eow), 0, 0):
        copy.wait()
    eq[...] = nn(emb[...], eqw[...]).astype(BF16)
    for h in range(enc_heads):
        cols = slice(h * HEAD, (h + 1) * HEAD)
        vcols = slice(width + h * HEAD, width + (h + 1) * HEAD)
        for b in range(count):
            rows = slice(b * nbr, (b + 1) * nbr)
            toks = slice(b * BLOCK, (b + 1) * BLOCK)
            probs = softmax_rows(nt(eq[rows, cols], mem[toks, cols]) * SCALE)
            probs_buf[h * count + b] = probs
            att[rows, cols] = nn(probs.astype(BF16), mem[toks, vcols]).astype(BF16)
    encoded = (emb[...].astype(F32) + nn(att[...], eow[...])).astype(BF16)
    for copy in loads(wide_refs, (kw, vw), 2 * dps, 0):
        copy.wait()
    keys[...] = nn(encoded, kw[...]).astype(BF16)
    values[...] = nn(encoded, vw[...]).astype(BF16)

    wide = kw.shape[1]
    tokens = count * BLOCK
    row = lax.broadcasted_iota(jnp.int32, (tokens, HEAD), 0)

    def grouped(ref, cols, halo_cols):
        moved = jnp.concatenate([ref[BLOCK:, cols], halo[:, halo_cols]], axis=0).astype(F32)
        first = ref[:BLOCK, cols].astype(F32)[BLOCK - 1 :]
        return jnp.where(row == 0, first, pltpu.roll(moved, 1, 0)).astype(BF16)

    def head(h, carry):
        start = pl.multiple_of(h * HEAD, HEAD)
        cols, more = pl.ds(start, HEAD), pl.ds(wide + start, HEAD)
        qs, gs = grouped(rq, cols, cols), grouped(rc, cols, more)
        ctx, grad = [], []
        for b in range(count):
            rows = slice(b * nbr, (b + 1) * nbr)
            toks = slice(b * BLOCK, (b + 1) * BLOCK)
            q, g, k, v = qs[toks], gs[toks], keys[rows, cols], values[rows, cols]
            probs = softmax_rows(nt(q, k) * SCALE)
            weights = probs.astype(BF16)
            ctx.append(nn(weights, v))
            d_probs = nt(g, v)
            centred = d_probs - jnp.sum(probs * d_probs, axis=-1, keepdims=True)
            d_scores = (probs * centred * SCALE).astype(BF16)
            grad.append(nn(d_scores, k))
            dkeys[rows, cols] = tn(d_scores, q).astype(BF16)
            dvalues[rows, cols] = tn(weights, g).astype(BF16)
        for parts, out, back in ((ctx, ctx_out, cols), (grad, grad_out, more)):
            turned = pltpu.roll(jnp.concatenate(parts, axis=0), BLOCK - 1, 0).astype(BF16)
            out[:, cols] = turned
            back_out[:, back] = turned[:BLOCK]
        return carry

    lax.fori_loop(0, heads, head, 0, unroll=4)
    enc_grad = (nt(dkeys[...], kw[...]) + nt(dvalues[...], vw[...])).astype(BF16)
    att[...] = nt(enc_grad, eow[...]).astype(BF16)
    for h in range(enc_heads):
        cols = slice(h * HEAD, (h + 1) * HEAD)
        vcols = slice(width + h * HEAD, width + (h + 1) * HEAD)
        for b in range(count):
            rows = slice(b * nbr, (b + 1) * nbr)
            toks = slice(b * BLOCK, (b + 1) * BLOCK)
            probs = probs_buf[h * count + b]
            grad = att[rows, cols]
            inner = nt(grad, mem[toks, vcols])
            centred = inner - jnp.sum(probs * inner, axis=-1, keepdims=True)
            d_scores = (probs * centred * SCALE).astype(BF16)
            mem_out[toks, cols] = tn(d_scores, eq[rows, cols]).astype(BF16)
            mem_out[toks, vcols] = tn(probs.astype(BF16), grad).astype(BF16)


def math_all(nbr, embt, mem, rq, rc, halo, enc, wides):
    width, tokens = embt.shape
    count = mem.shape[0] // BLOCK
    wide = rq.shape[1]
    dps = lax.axis_size("dp")
    anywhere = pl.BlockSpec(memory_space=pl.ANY)
    vmem = pl.BlockSpec(memory_space=pltpu.VMEM)
    shape = jax.ShapeDtypeStruct
    return pl.pallas_call(
        functools.partial(math_kernel, nbr, dps),
        out_shape=[shape(a.shape, BF16) for a in (rq, rc, halo, mem)],
        in_specs=[vmem] * 5 + [anywhere] * (4 * dps),
        out_specs=[vmem] * 4,
        scratch_shapes=[
            pltpu.VMEM((width, width), BF16),
            pltpu.VMEM((width, width), BF16),
            pltpu.VMEM((width, wide), BF16),
            pltpu.VMEM((width, wide), BF16),
            pltpu.SemaphoreType.DMA((4 * dps,)),
            pltpu.VMEM((tokens, width), BF16),
            pltpu.VMEM((tokens, width), BF16),
            pltpu.VMEM((tokens, width), BF16),
            pltpu.VMEM((width // HEAD * count, nbr, BLOCK), F32),
        ]
        + [pltpu.VMEM((tokens, wide), BF16)] * 4,
    )(embt, mem, rq, rc, halo, *enc, *wides)


def body(
    queries,
    block_memory,
    neighbour_ids,
    embedding,
    enc_query_w,
    enc_out_w,
    key_w,
    value_w,
    context_cot,
):
    q, mem, ids, cot = queries[0], block_memory[0], neighbour_ids[0], context_cot[0]
    tokens, wide = q.shape
    nbr = ids.shape[1]
    seqs = lax.axis_size("seq")
    enc = spread((enc_query_w, enc_out_w))
    wides = spread((key_w, value_w))
    edge = jnp.concatenate([q[:BLOCK], cot[:BLOCK]], axis=1)
    halo = lax.ppermute(edge, "seq", [(s + 1, s) for s in range(seqs - 1)])
    stage = look_up(share_ids(ids), embedding)
    emb = swap_features(stage)
    ctx, grad, back, mem_grad = math_all(
        nbr, emb.reshape(-1, emb.shape[2]), mem, q, cot, halo, enc, wides
    )
    back = lax.ppermute(back, "seq", [(s, s + 1) for s in range(seqs - 1)])
    behind = lax.broadcasted_iota(jnp.int32, (BLOCK, wide), 0) < BLOCK - 1
    context = ctx.at[:BLOCK].set(jnp.where(behind, back[:, :wide], ctx[:BLOCK]))
    query_grad = grad.at[:BLOCK].set(jnp.where(behind, back[:, wide:], grad[:BLOCK]))
    return (context[None], query_grad[None], mem_grad[None])


def solution(mesh):
    rows = P("dp", "seq", None)
    split = P("dp", None)
    return jax.shard_map(
        body,
        mesh=mesh,
        in_specs=(rows, rows, rows, P("seq", None), split, split, split, split, rows),
        out_specs=(rows, rows, rows),
        check_vma=False,
    )
```

```python
import functools

import jax
import jax.numpy as jnp
from jax import lax
from jax.experimental import pallas as pl
from jax.experimental.pallas import tpu as pltpu
from jax.sharding import PartitionSpec as P

HEAD = 128
BLOCK = 64
SCALE = HEAD ** (-0.5)
F32 = jnp.float32
BF16 = jnp.bfloat16
MESH = pl.DeviceIdType.MESH


def cost(flops):
    return pl.CostEstimate(flops=flops, bytes_accessed=0, transcendentals=0)


def ids_kernel(seqs, ids_ref, ids_out, send, recv, local):
    dp = lax.axis_index("dp")
    sq = lax.axis_index("seq")
    own = pltpu.make_async_copy(ids_ref, ids_out.at[sq], local)
    own.start()
    barrier = pltpu.get_barrier_semaphore()
    for k in range(1, seqs):
        pl.semaphore_signal(
            barrier, inc=1, device_id=(dp, lax.rem(sq + k, seqs)), device_id_type=MESH
        )
    pl.semaphore_wait(barrier, seqs - 1)

    copies = []
    for k in range(1, seqs):
        copies.append(
            pltpu.make_async_remote_copy(
                src_ref=ids_ref,
                dst_ref=ids_out.at[sq],
                send_sem=send.at[k],
                recv_sem=recv.at[k],
                device_id=(dp, lax.rem(sq + k, seqs)),
                device_id_type=MESH,
            )
        )
        copies[-1].start()
    own.wait()
    for copy in copies:
        copy.wait()


def share_ids(ids):
    seqs = lax.axis_size("seq")
    anywhere = pl.BlockSpec(memory_space=pl.ANY)
    dma = pltpu.SemaphoreType.DMA
    return pl.pallas_call(
        functools.partial(ids_kernel, seqs),
        out_shape=jax.ShapeDtypeStruct((seqs,) + ids.shape, jnp.int32),
        in_specs=[anywhere],
        out_specs=anywhere,
        scratch_shapes=[dma((seqs,)), dma((seqs,)), dma],
        cost_estimate=cost(6 * 10**9),
        compiler_params=pltpu.CompilerParams(collective_id=1, has_side_effects=True),
    )(ids)


def look_kernel(ids, table, out):
    seqs, count, nbr = ids.shape
    feats = table.shape[0]
    lane = lax.broadcasted_iota(jnp.int32, (feats, HEAD), 1)
    step = 32

    def chunk(to, carry):
        for b in range(count):
            for part in range(nbr // HEAD):

                def some(i, acc):
                    for t in range(step):
                        j = i * step + t
                        token = ids[to, b, part * HEAD + j]
                        start = pl.multiple_of((token >> 7) << 7, HEAD)
                        tile = table[:, pl.ds(start, HEAD)].astype(F32)
                        moved = pltpu.roll(tile, (j - token) & (HEAD - 1), 1)
                        acc = jnp.where(lane == j, moved, acc)
                    return acc

                acc = lax.fori_loop(0, HEAD // step, some, jnp.zeros((feats, HEAD), F32))
                first = b * nbr + part * HEAD
                out[to, :, first : first + HEAD] = acc.astype(BF16)
        return carry

    lax.fori_loop(0, seqs, chunk, 0)


def look_up(ids, table):
    seqs, count, nbr = ids.shape
    feats = table.shape[0]
    return pl.pallas_call(
        look_kernel,
        out_shape=jax.ShapeDtypeStruct((seqs, feats, count * nbr), BF16),
        in_specs=[
            pl.BlockSpec(memory_space=pltpu.SMEM),
            pl.BlockSpec(memory_space=pltpu.VMEM),
        ],
        out_specs=pl.BlockSpec(memory_space=pltpu.VMEM),
        cost_estimate=cost(26 * 10**9),
    )(ids, table)


def swap_kernel(seqs, stage, emb_out, send, recv, local):
    dp = lax.axis_index("dp")
    sq = lax.axis_index("seq")
    own = pltpu.make_async_copy(stage.at[sq], emb_out.at[sq], local)
    own.start()
    barrier = pltpu.get_barrier_semaphore()
    for k in range(1, seqs):
        pl.semaphore_signal(
            barrier, inc=1, device_id=(dp, lax.rem(sq + k, seqs)), device_id_type=MESH
        )
    pl.semaphore_wait(barrier, seqs - 1)
    copies = []
    for k in range(1, seqs):
        to = lax.rem(sq + k, seqs)
        copies.append(
            pltpu.make_async_remote_copy(
                src_ref=stage.at[to],
                dst_ref=emb_out.at[sq],
                send_sem=send.at[k],
                recv_sem=recv.at[k],
                device_id=(dp, to),
                device_id_type=MESH,
            )
        )
        copies[-1].start()
    own.wait()
    for copy in copies:
        copy.wait()


def swap_features(stage):
    seqs = lax.axis_size("seq")
    anywhere = pl.BlockSpec(memory_space=pl.ANY)
    dma = pltpu.SemaphoreType.DMA
    return pl.pallas_call(
        functools.partial(swap_kernel, seqs),
        out_shape=jax.ShapeDtypeStruct(stage.shape, BF16),
        in_specs=[anywhere],
        out_specs=anywhere,
        scratch_shapes=[dma((seqs,)), dma((seqs,)), dma],
        cost_estimate=cost(12 * 10**9),
        compiler_params=pltpu.CompilerParams(collective_id=0, has_side_effects=True),
    )(stage)


def spread(pair):
    dps, seqs = lax.axis_size("dp"), lax.axis_size("seq")
    mine = jnp.where(lax.axis_index("seq") % 2 == 0, pair[0], pair[1])
    fetched = [
        lax.ppermute(mine, "dp", [(s, (s + k) % dps) for s in range(dps)]) for k in range(1, dps)
    ]
    return fetched


def pass_on(fetched):
    seqs = lax.axis_size("seq")
    return [lax.ppermute(f, "seq", [(s, s ^ 1) for s in range(seqs)]) for f in fetched]


def nt(a, b):
    return lax.dot_general(a, b, (((1,), (1,)), ((), ())), preferred_element_type=F32)


def nn(a, b):
    return lax.dot_general(a, b, (((1,), (0,)), ((), ())), preferred_element_type=F32)


def tn(a, b):
    return lax.dot_general(a, b, (((0,), (0,)), ((), ())), preferred_element_type=F32)


def softmax_rows(scores):
    top = jnp.max(scores, axis=-1, keepdims=True)
    expo = jnp.exp(scores - top)
    return expo / jnp.sum(expo, axis=-1, keepdims=True)


def math_kernel(nbr, dps, embt, mem, rq, rc, halo, *refs):
    pieces = 2 * dps
    enc_refs, wide_refs = refs[:pieces], refs[pieces : 2 * pieces]
    math_inner(nbr, dps, enc_refs, wide_refs, embt, mem, rq, rc, halo, *refs[2 * pieces :])


def math_inner(
    nbr,
    dps,
    enc_refs,
    wide_refs,
    embt,
    mem,
    rq,
    rc,
    halo,
    ctx_out,
    grad_out,
    back_out,
    mem_out,
    eqw,
    eow,
    kw,
    vw,
    sems,
    emb,
    eq,
    att,
    probs_buf,
    keys,
    values,
    dkeys,
    dvalues,
):
    count = mem.shape[0] // BLOCK
    width = eqw.shape[0]
    enc_heads = width // HEAD
    heads = kw.shape[1] // HEAD
    dp = lax.axis_index("dp")
    core = lax.rem(lax.axis_index("seq"), 2)

    def loads(refs, pair, base, side):
        piece = refs[0].shape[0]
        copies = []
        for i, ref in enumerate(refs):
            if i < 2:
                target, owner = pair[i], dp
            elif i < dps + 1:
                target, owner = pair[side], lax.rem(dp - (i - 1) + dps, dps)
            else:
                target, owner = pair[1 - side], lax.rem(dp - (i - dps) + dps, dps)
            rows = pl.ds(pl.multiple_of(owner * piece, 8), piece)
            copies.append(pltpu.make_async_copy(ref, target.at[rows], sems.at[base + i]))
        return copies

    for side in range(2):

        @pl.when(core == side)
        def _():
            for copy in loads(enc_refs, (eqw, eow), 0, side):
                copy.start()
            for copy in loads(wide_refs, (kw, vw), 2 * dps, side):
                copy.start()

    emb[...] = embt[...].T
    for copy in loads(enc_refs, (eqw, eow), 0, 0):
        copy.wait()
    eq[...] = nn(emb[...], eqw[...]).astype(BF16)
    for h in range(enc_heads):
        cols = slice(h * HEAD, (h + 1) * HEAD)
        vcols = slice(width + h * HEAD, width + (h + 1) * HEAD)
        for b in range(count):
            rows = slice(b * nbr, (b + 1) * nbr)
            toks = slice(b * BLOCK, (b + 1) * BLOCK)
            probs = softmax_rows(nt(eq[rows, cols], mem[toks, cols]) * SCALE)
            probs_buf[h * count + b] = probs
            att[rows, cols] = nn(probs.astype(BF16), mem[toks, vcols]).astype(BF16)
    encoded = (emb[...].astype(F32) + nn(att[...], eow[...])).astype(BF16)
    for copy in loads(wide_refs, (kw, vw), 2 * dps, 0):
        copy.wait()
    keys[...] = nn(encoded, kw[...]).astype(BF16)
    values[...] = nn(encoded, vw[...]).astype(BF16)

    wide = kw.shape[1]
    tokens = count * BLOCK
    row = lax.broadcasted_iota(jnp.int32, (tokens, HEAD), 0)

    def grouped(ref, cols, halo_cols):
        moved = jnp.concatenate([ref[BLOCK:, cols], halo[:, halo_cols]], axis=0).astype(F32)
        first = ref[:BLOCK, cols].astype(F32)[BLOCK - 1 :]
        return jnp.where(row == 0, first, pltpu.roll(moved, 1, 0)).astype(BF16)

    def head(h, carry):
        start = pl.multiple_of(h * HEAD, HEAD)
        cols, more = pl.ds(start, HEAD), pl.ds(wide + start, HEAD)
        qs, gs = grouped(rq, cols, cols), grouped(rc, cols, more)
        ctx, grad = [], []
        for b in range(count):
            rows = slice(b * nbr, (b + 1) * nbr)
            toks = slice(b * BLOCK, (b + 1) * BLOCK)
            q, g, k, v = qs[toks], gs[toks], keys[rows, cols], values[rows, cols]
            probs = softmax_rows(nt(q, k) * SCALE)
            weights = probs.astype(BF16)
            ctx.append(nn(weights, v))
            d_probs = nt(g, v)
            centred = d_probs - jnp.sum(probs * d_probs, axis=-1, keepdims=True)
            d_scores = (probs * centred * SCALE).astype(BF16)
            grad.append(nn(d_scores, k))
            dkeys[rows, cols] = tn(d_scores, q).astype(BF16)
            dvalues[rows, cols] = tn(weights, g).astype(BF16)
        for parts, out, back in ((ctx, ctx_out, cols), (grad, grad_out, more)):
            turned = pltpu.roll(jnp.concatenate(parts, axis=0), BLOCK - 1, 0).astype(BF16)
            out[:, cols] = turned
            back_out[:, back] = turned[:BLOCK]
        return carry

    lax.fori_loop(0, heads, head, 0, unroll=4)
    enc_grad = (nt(dkeys[...], kw[...]) + nt(dvalues[...], vw[...])).astype(BF16)
    att[...] = nt(enc_grad, eow[...]).astype(BF16)
    for h in range(enc_heads):
        cols = slice(h * HEAD, (h + 1) * HEAD)
        vcols = slice(width + h * HEAD, width + (h + 1) * HEAD)
        for b in range(count):
            rows = slice(b * nbr, (b + 1) * nbr)
            toks = slice(b * BLOCK, (b + 1) * BLOCK)
            probs = probs_buf[h * count + b]
            grad = att[rows, cols]
            inner = nt(grad, mem[toks, vcols])
            centred = inner - jnp.sum(probs * inner, axis=-1, keepdims=True)
            d_scores = (probs * centred * SCALE).astype(BF16)
            mem_out[toks, cols] = tn(d_scores, eq[rows, cols]).astype(BF16)
            mem_out[toks, vcols] = tn(probs.astype(BF16), grad).astype(BF16)


def math_all(nbr, embt, mem, rq, rc, halo, enc, wides):
    width, tokens = embt.shape
    count = mem.shape[0] // BLOCK
    wide = rq.shape[1]
    dps = lax.axis_size("dp")
    anywhere = pl.BlockSpec(memory_space=pl.ANY)
    vmem = pl.BlockSpec(memory_space=pltpu.VMEM)
    shape = jax.ShapeDtypeStruct
    return pl.pallas_call(
        functools.partial(math_kernel, nbr, dps),
        out_shape=[shape(a.shape, BF16) for a in (rq, rc, halo, mem)],
        in_specs=[vmem] * 5 + [anywhere] * (4 * dps),
        out_specs=[vmem] * 4,
        scratch_shapes=[
            pltpu.VMEM((width, width), BF16),
            pltpu.VMEM((width, width), BF16),
            pltpu.VMEM((width, wide), BF16),
            pltpu.VMEM((width, wide), BF16),
            pltpu.SemaphoreType.DMA((4 * dps,)),
            pltpu.VMEM((tokens, width), BF16),
            pltpu.VMEM((tokens, width), BF16),
            pltpu.VMEM((tokens, width), BF16),
            pltpu.VMEM((width // HEAD * count, nbr, BLOCK), F32),
        ]
        + [pltpu.VMEM((tokens, wide), BF16)] * 4,
    )(embt, mem, rq, rc, halo, *enc, *wides)


def body(
    queries,
    block_memory,
    neighbour_ids,
    embedding,
    enc_query_w,
    enc_out_w,
    key_w,
    value_w,
    context_cot,
):
    q, mem, ids, cot = queries[0], block_memory[0], neighbour_ids[0], context_cot[0]
    tokens, wide = q.shape
    nbr = ids.shape[1]
    seqs = lax.axis_size("seq")
    enc = spread((enc_query_w, enc_out_w))
    wides = spread((key_w, value_w))
    edge = jnp.concatenate([q[:BLOCK], cot[:BLOCK]], axis=1)
    halo = lax.ppermute(edge, "seq", [(s + 1, s) for s in range(seqs - 1)])
    stage = look_up(share_ids(ids), embedding)
    wides, stage = lax.optimization_barrier((wides, stage))
    wides = [key_w, value_w] + wides + pass_on(wides)
    emb = swap_features(stage)
    enc, emb = lax.optimization_barrier((enc, emb))
    enc = [enc_query_w, enc_out_w] + enc + pass_on(enc)
    ctx, grad, back, mem_grad = math_all(
        nbr, emb.reshape(-1, emb.shape[2]), mem, q, cot, halo, enc, wides
    )
    back = lax.ppermute(back, "seq", [(s, s + 1) for s in range(seqs - 1)])
    behind = lax.broadcasted_iota(jnp.int32, (BLOCK, wide), 0) < BLOCK - 1
    context = ctx.at[:BLOCK].set(jnp.where(behind, back[:, :wide], ctx[:BLOCK]))
    query_grad = grad.at[:BLOCK].set(jnp.where(behind, back[:, wide:], grad[:BLOCK]))
    return (context[None], query_grad[None], mem_grad[None])


def solution(mesh):
    rows = P("dp", "seq", None)
    split = P("dp", None)
    return jax.shard_map(
        body,
        mesh=mesh,
        in_specs=(rows, rows, rows, P("seq", None), split, split, split, split, rows),
        out_specs=(rows, rows, rows),
        check_vma=False,
    )
```

```python
import functools

import jax
import jax.numpy as jnp
from jax import lax
from jax.experimental import pallas as pl
from jax.experimental.pallas import tpu as pltpu
from jax.sharding import PartitionSpec as P

HEAD = 128
BLOCK = 64
SCALE = HEAD ** (-0.5)
F32 = jnp.float32
BF16 = jnp.bfloat16
MESH = pl.DeviceIdType.MESH


def cost(flops):
    return pl.CostEstimate(flops=flops, bytes_accessed=0, transcendentals=0)


def ids_kernel(seqs, ids_ref, ids_out, send, recv, local):
    dp = lax.axis_index("dp")
    sq = lax.axis_index("seq")
    own = pltpu.make_async_copy(ids_ref, ids_out.at[sq], local)
    own.start()
    barrier = pltpu.get_barrier_semaphore()
    for k in range(1, seqs):
        pl.semaphore_signal(
            barrier, inc=1, device_id=(dp, lax.rem(sq + k, seqs)), device_id_type=MESH
        )
    pl.semaphore_wait(barrier, seqs - 1)

    copies = []
    for k in range(1, seqs):
        copies.append(
            pltpu.make_async_remote_copy(
                src_ref=ids_ref,
                dst_ref=ids_out.at[sq],
                send_sem=send.at[k],
                recv_sem=recv.at[k],
                device_id=(dp, lax.rem(sq + k, seqs)),
                device_id_type=MESH,
            )
        )
        copies[-1].start()
    own.wait()
    for copy in copies:
        copy.wait()


def share_ids(ids):
    seqs = lax.axis_size("seq")
    anywhere = pl.BlockSpec(memory_space=pl.ANY)
    dma = pltpu.SemaphoreType.DMA
    return pl.pallas_call(
        functools.partial(ids_kernel, seqs),
        out_shape=jax.ShapeDtypeStruct((seqs,) + ids.shape, jnp.int32),
        in_specs=[anywhere],
        out_specs=anywhere,
        scratch_shapes=[dma((seqs,)), dma((seqs,)), dma],
        cost_estimate=cost(6 * 10**9),
        compiler_params=pltpu.CompilerParams(collective_id=1, has_side_effects=True),
    )(ids)


def look_kernel(ids, table, out):
    seqs, count, nbr = ids.shape
    feats = table.shape[0]
    lane = lax.broadcasted_iota(jnp.int32, (feats, HEAD), 1)
    step = 64

    def chunk(to, carry):
        for b in range(count):
            for part in range(nbr // HEAD):

                def some(i, acc):
                    for t in range(step):
                        j = i * step + t
                        token = ids[to, b, part * HEAD + j]
                        start = pl.multiple_of((token >> 7) << 7, HEAD)
                        tile = table[:, pl.ds(start, HEAD)].astype(F32)
                        moved = pltpu.roll(tile, (j - token) & (HEAD - 1), 1)
                        acc = jnp.where(lane == j, moved, acc)
                    return acc

                acc = lax.fori_loop(0, HEAD // step, some, jnp.zeros((feats, HEAD), F32))
                first = b * nbr + part * HEAD
                out[to, :, first : first + HEAD] = acc.astype(BF16)
        return carry

    lax.fori_loop(0, seqs, chunk, 0)


def look_up(ids, table):
    seqs, count, nbr = ids.shape
    feats = table.shape[0]
    return pl.pallas_call(
        look_kernel,
        out_shape=jax.ShapeDtypeStruct((seqs, feats, count * nbr), BF16),
        in_specs=[
            pl.BlockSpec(memory_space=pltpu.SMEM),
            pl.BlockSpec(memory_space=pltpu.VMEM),
        ],
        out_specs=pl.BlockSpec(memory_space=pltpu.VMEM),
        cost_estimate=cost(26 * 10**9),
    )(ids, table)


def swap_kernel(seqs, stage, emb_out, send, recv, local):
    dp = lax.axis_index("dp")
    sq = lax.axis_index("seq")
    own = pltpu.make_async_copy(stage.at[sq], emb_out.at[sq], local)
    own.start()
    barrier = pltpu.get_barrier_semaphore()
    for k in range(1, seqs):
        pl.semaphore_signal(
            barrier, inc=1, device_id=(dp, lax.rem(sq + k, seqs)), device_id_type=MESH
        )
    pl.semaphore_wait(barrier, seqs - 1)
    copies = []
    for k in range(1, seqs):
        to = lax.rem(sq + k, seqs)
        copies.append(
            pltpu.make_async_remote_copy(
                src_ref=stage.at[to],
                dst_ref=emb_out.at[sq],
                send_sem=send.at[k],
                recv_sem=recv.at[k],
                device_id=(dp, to),
                device_id_type=MESH,
            )
        )
        copies[-1].start()
    own.wait()
    for copy in copies:
        copy.wait()


def swap_features(stage):
    seqs = lax.axis_size("seq")
    anywhere = pl.BlockSpec(memory_space=pl.ANY)
    dma = pltpu.SemaphoreType.DMA
    return pl.pallas_call(
        functools.partial(swap_kernel, seqs),
        out_shape=jax.ShapeDtypeStruct(stage.shape, BF16),
        in_specs=[anywhere],
        out_specs=anywhere,
        scratch_shapes=[dma((seqs,)), dma((seqs,)), dma],
        cost_estimate=cost(12 * 10**9),
        compiler_params=pltpu.CompilerParams(collective_id=0, has_side_effects=True),
    )(stage)


def spread(pair):
    dps, seqs = lax.axis_size("dp"), lax.axis_size("seq")
    mine = jnp.where(lax.axis_index("seq") % 2 == 0, pair[0], pair[1])
    fetched = [
        lax.ppermute(mine, "dp", [(s, (s + k) % dps) for s in range(dps)]) for k in range(1, dps)
    ]
    return fetched


def pass_on(fetched):
    seqs = lax.axis_size("seq")
    return [lax.ppermute(f, "seq", [(s, s ^ 1) for s in range(seqs)]) for f in fetched]


def nt(a, b):
    return lax.dot_general(a, b, (((1,), (1,)), ((), ())), preferred_element_type=F32)


def nn(a, b):
    return lax.dot_general(a, b, (((1,), (0,)), ((), ())), preferred_element_type=F32)


def tn(a, b):
    return lax.dot_general(a, b, (((0,), (0,)), ((), ())), preferred_element_type=F32)


def softmax_rows(scores):
    top = jnp.max(scores, axis=-1, keepdims=True)
    expo = jnp.exp(scores - top)
    return expo / jnp.sum(expo, axis=-1, keepdims=True)


def math_kernel(nbr, dps, embt, mem, rq, rc, halo, *refs):
    pieces = 2 * dps
    enc_refs, wide_refs = refs[:pieces], refs[pieces : 2 * pieces]
    math_inner(nbr, dps, enc_refs, wide_refs, embt, mem, rq, rc, halo, *refs[2 * pieces :])


def math_inner(
    nbr,
    dps,
    enc_refs,
    wide_refs,
    embt,
    mem,
    rq,
    rc,
    halo,
    ctx_out,
    grad_out,
    back_out,
    mem_out,
    eqw,
    eow,
    kw,
    vw,
    sems,
    emb,
    eq,
    att,
    probs_buf,
    keys,
    values,
    dkeys,
    dvalues,
):
    count = mem.shape[0] // BLOCK
    width = eqw.shape[0]
    enc_heads = width // HEAD
    heads = kw.shape[1] // HEAD
    dp = lax.axis_index("dp")
    core = lax.rem(lax.axis_index("seq"), 2)

    def loads(refs, pair, base, side):
        piece = refs[0].shape[0]
        copies = []
        for i, ref in enumerate(refs):
            if i < 2:
                target, owner = pair[i], dp
            elif i < dps + 1:
                target, owner = pair[side], lax.rem(dp - (i - 1) + dps, dps)
            else:
                target, owner = pair[1 - side], lax.rem(dp - (i - dps) + dps, dps)
            rows = pl.ds(pl.multiple_of(owner * piece, 8), piece)
            copies.append(pltpu.make_async_copy(ref, target.at[rows], sems.at[base + i]))
        return copies

    for side in range(2):

        @pl.when(core == side)
        def _():
            for copy in loads(enc_refs, (eqw, eow), 0, side):
                copy.start()
            for copy in loads(wide_refs, (kw, vw), 2 * dps, side):
                copy.start()

    emb[...] = embt[...].T
    for copy in loads(enc_refs, (eqw, eow), 0, 0):
        copy.wait()
    eq[...] = nn(emb[...], eqw[...]).astype(BF16)
    for h in range(enc_heads):
        cols = slice(h * HEAD, (h + 1) * HEAD)
        vcols = slice(width + h * HEAD, width + (h + 1) * HEAD)
        for b in range(count):
            rows = slice(b * nbr, (b + 1) * nbr)
            toks = slice(b * BLOCK, (b + 1) * BLOCK)
            probs = softmax_rows(nt(eq[rows, cols], mem[toks, cols]) * SCALE)
            probs_buf[h * count + b] = probs
            att[rows, cols] = nn(probs.astype(BF16), mem[toks, vcols]).astype(BF16)
    encoded = (emb[...].astype(F32) + nn(att[...], eow[...])).astype(BF16)
    for copy in loads(wide_refs, (kw, vw), 2 * dps, 0):
        copy.wait()
    keys[...] = nn(encoded, kw[...]).astype(BF16)
    values[...] = nn(encoded, vw[...]).astype(BF16)

    wide = kw.shape[1]
    tokens = count * BLOCK
    row = lax.broadcasted_iota(jnp.int32, (tokens, HEAD), 0)

    def grouped(ref, cols, halo_cols):
        moved = jnp.concatenate([ref[BLOCK:, cols], halo[:, halo_cols]], axis=0).astype(F32)
        first = ref[:BLOCK, cols].astype(F32)[BLOCK - 1 :]
        return jnp.where(row == 0, first, pltpu.roll(moved, 1, 0)).astype(BF16)

    def head(h, carry):
        start = pl.multiple_of(h * HEAD, HEAD)
        cols, more = pl.ds(start, HEAD), pl.ds(wide + start, HEAD)
        qs, gs = grouped(rq, cols, cols), grouped(rc, cols, more)
        ctx, grad = [], []
        for b in range(count):
            rows = slice(b * nbr, (b + 1) * nbr)
            toks = slice(b * BLOCK, (b + 1) * BLOCK)
            q, g, k, v = qs[toks], gs[toks], keys[rows, cols], values[rows, cols]
            probs = softmax_rows(nt(q, k) * SCALE)
            weights = probs.astype(BF16)
            ctx.append(nn(weights, v))
            d_probs = nt(g, v)
            centred = d_probs - jnp.sum(probs * d_probs, axis=-1, keepdims=True)
            d_scores = (probs * centred * SCALE).astype(BF16)
            grad.append(nn(d_scores, k))
            dkeys[rows, cols] = tn(d_scores, q).astype(BF16)
            dvalues[rows, cols] = tn(weights, g).astype(BF16)
        for parts, out, back in ((ctx, ctx_out, cols), (grad, grad_out, more)):
            turned = pltpu.roll(jnp.concatenate(parts, axis=0), BLOCK - 1, 0).astype(BF16)
            out[:, cols] = turned
            back_out[:, back] = turned[:BLOCK]
        return carry

    lax.fori_loop(0, heads, head, 0, unroll=8)
    enc_grad = (nt(dkeys[...], kw[...]) + nt(dvalues[...], vw[...])).astype(BF16)
    att[...] = nt(enc_grad, eow[...]).astype(BF16)
    for h in range(enc_heads):
        cols = slice(h * HEAD, (h + 1) * HEAD)
        vcols = slice(width + h * HEAD, width + (h + 1) * HEAD)
        for b in range(count):
            rows = slice(b * nbr, (b + 1) * nbr)
            toks = slice(b * BLOCK, (b + 1) * BLOCK)
            probs = probs_buf[h * count + b]
            grad = att[rows, cols]
            inner = nt(grad, mem[toks, vcols])
            centred = inner - jnp.sum(probs * inner, axis=-1, keepdims=True)
            d_scores = (probs * centred * SCALE).astype(BF16)
            mem_out[toks, cols] = tn(d_scores, eq[rows, cols]).astype(BF16)
            mem_out[toks, vcols] = tn(probs.astype(BF16), grad).astype(BF16)


def math_all(nbr, embt, mem, rq, rc, halo, enc, wides):
    width, tokens = embt.shape
    count = mem.shape[0] // BLOCK
    wide = rq.shape[1]
    dps = lax.axis_size("dp")
    anywhere = pl.BlockSpec(memory_space=pl.ANY)
    vmem = pl.BlockSpec(memory_space=pltpu.VMEM)
    shape = jax.ShapeDtypeStruct
    return pl.pallas_call(
        functools.partial(math_kernel, nbr, dps),
        out_shape=[shape(a.shape, BF16) for a in (rq, rc, halo, mem)],
        in_specs=[vmem] * 5 + [anywhere] * (4 * dps),
        out_specs=[vmem] * 4,
        scratch_shapes=[
            pltpu.VMEM((width, width), BF16),
            pltpu.VMEM((width, width), BF16),
            pltpu.VMEM((width, wide), BF16),
            pltpu.VMEM((width, wide), BF16),
            pltpu.SemaphoreType.DMA((4 * dps,)),
            pltpu.VMEM((tokens, width), BF16),
            pltpu.VMEM((tokens, width), BF16),
            pltpu.VMEM((tokens, width), BF16),
            pltpu.VMEM((width // HEAD * count, nbr, BLOCK), F32),
        ]
        + [pltpu.VMEM((tokens, wide), BF16)] * 4,
    )(embt, mem, rq, rc, halo, *enc, *wides)


def body(
    queries,
    block_memory,
    neighbour_ids,
    embedding,
    enc_query_w,
    enc_out_w,
    key_w,
    value_w,
    context_cot,
):
    q, mem, ids, cot = queries[0], block_memory[0], neighbour_ids[0], context_cot[0]
    tokens, wide = q.shape
    nbr = ids.shape[1]
    seqs = lax.axis_size("seq")
    enc = spread((enc_query_w, enc_out_w))
    wides = spread((key_w, value_w))
    edge = jnp.concatenate([q[:BLOCK], cot[:BLOCK]], axis=1)
    all_ids, edge = lax.optimization_barrier((share_ids(ids), edge))
    halo = lax.ppermute(edge, "seq", [(s + 1, s) for s in range(seqs - 1)])
    stage = look_up(all_ids, embedding)
    wides, stage = lax.optimization_barrier((wides, stage))
    wides = [key_w, value_w] + wides + pass_on(wides)
    emb = swap_features(stage)
    enc, emb = lax.optimization_barrier((enc, emb))
    enc = [enc_query_w, enc_out_w] + enc + pass_on(enc)
    ctx, grad, back, mem_grad = math_all(
        nbr, emb.reshape(-1, emb.shape[2]), mem, q, cot, halo, enc, wides
    )
    back = lax.ppermute(back, "seq", [(s, s + 1) for s in range(seqs - 1)])
    behind = lax.broadcasted_iota(jnp.int32, (BLOCK, wide), 0) < BLOCK - 1
    context = ctx.at[:BLOCK].set(jnp.where(behind, back[:, :wide], ctx[:BLOCK]))
    query_grad = grad.at[:BLOCK].set(jnp.where(behind, back[:, wide:], grad[:BLOCK]))
    return (context[None], query_grad[None], mem_grad[None])


def solution(mesh):
    rows = P("dp", "seq", None)
    split = P("dp", None)
    return jax.shard_map(
        body,
        mesh=mesh,
        in_specs=(rows, rows, rows, P("seq", None), split, split, split, split, rows),
        out_specs=(rows, rows, rows),
        check_vma=False,
    )
```
